128 devices in a mesh: dp: 16 (over x, z_hi, core), head: 8 (over z_lo, y).
Axes of the slice: x: 4, y: 4, z: 4 (z_hi: 2, z_lo: 2; z = z_hi * 2 + z_lo), core: 2. Of those that a mesh axis runs over, the one named last changes fastest.
Arguments:
- latent: bfloat16 [16384, 512], P(('dp', 'head')), may hold values from -32 to 32
- out_grad: bfloat16 [16384, 16, 8, 256], P('dp', None, 'head'), may hold values from -6 to 6
- weight: float32 [512, 16, 8, 256], P(None, 'dp', 'head'), may hold values from -0.25 to 0.25
- moment_one: float32 [512, 16, 8, 256], P(None, 'dp', 'head'), may hold values from -4 to 4
- moment_two: float32 [512, 16, 8, 256], P(None, 'dp', 'head'), may hold values from 0.1 to 2
Outputs:
- latent_grad: bfloat16 [16384, 512], P(('dp', 'head'))
- new_weight: float32 [512, 16, 8, 256], P(None, 'dp', 'head')
- new_moment_one: float32 [512, 16, 8, 256], P(None, 'dp', 'head')
- new_moment_two: float32 [512, 16, 8, 256], P(None, 'dp', 'head')
The draws below stay inside these ranges and needn't reach their ends.
All inputs are finite; a program needn't handle non-finite values.
Results may differ from the reference program's by a relative error of at most 0.014.
Values may be sent and summed in bfloat16 or wider, within the bound.
No kernel may reach another device: no remote copies, remote signals or barrier semaphores. Data moves between devices by JAX's collectives and lax.ppermute only.
A program may use at most 128 MiB of HBM per device.

```python
import math
import jax
import jax.numpy as jnp
from jax import lax

LATENT = 512
HEAD_COLS = 256
TOK_DEV = 1024
TOKENS = 16384
N_DP = 16
N_HEAD = 8


def draw_latent(key, part):
    base = jax.random.fold_in(key, 11)
    scale_key = jax.random.fold_in(base, 1)
    value_key = jax.random.fold_in(base, 2)
    channel_scale = jnp.exp(jax.random.uniform(scale_key, (LATENT,), jnp.float32, math.log(0.25), math.log(8.0)))
    values = jax.random.truncated_normal(value_key, -4.0, 4.0, (TOKENS, LATENT), jnp.float32)
    return (values * channel_scale[None, :]).astype(jnp.bfloat16)


def spiked(array, rng, source, target, parts, factor):
    def block_of(dim):
        return (jnp.arange(array.shape[dim]) // (array.shape[dim] // parts)).reshape((-1,) + (1,) * (array.ndim - 1 - dim))

    one_side = jax.random.permutation(rng, parts)[block_of(target)]
    second = (block_of(target) + parts // 2) % parts
    return jnp.where((block_of(source) == one_side) | (block_of(source) == second), factor * array, array)


def block_levels(rng, shape, pieces, low, high):
    def one(axis_at, blocks):
        heights = jax.random.uniform(jax.random.fold_in(jax.random.fold_in(rng, 6), axis_at), (blocks,), jnp.float32, low / len(pieces), high / len(pieces))
        return jnp.repeat(jnp.exp(heights), shape[axis_at] // blocks).reshape((-1,) + (1,) * (len(shape) - axis_at - 1))

    factor_of = one(*pieces[0])
    for cut in pieces[1:]:
        factor_of = factor_of * one(*cut)
    return factor_of


def bell_draw(stream_key, shape, width, bound, pieces=(), held_as=jnp.bfloat16):
    level = block_levels(stream_key, shape, pieces, -0.22, 0.18) if pieces else 1.0
    values = jax.random.normal(stream_key, shape, jnp.float32) * width * level
    return jnp.minimum(jnp.maximum(values, -bound), bound).astype(held_as)


def bell_draw_with(own_key, dims, scale, limit, cuts, heavy, kind=jnp.bfloat16):
    entries = scale * jax.random.normal(own_key, dims, jnp.float32)
    if cuts:
        entries = entries * block_levels(own_key, dims, cuts, -0.22, 0.18)
    return jnp.clip(spiked(entries, jax.random.fold_in(own_key, 3), *heavy), -limit, limit).astype(kind)


def setup_inputs(seed: int = 0) -> dict:
    key_list = jax.random.split(jax.random.key(seed), 6)
    return {
        "latent": draw_latent(jax.random.fold_in(key_list[5], 71), 0),
        "out_grad": bell_draw_with(key_list[1], (TOKENS, N_DP, N_HEAD, HEAD_COLS), 1.0, 6.0, ((0, 16), (2, 8)), (0, 1, 16, 2.0)),
        "weight": bell_draw(key_list[2], (LATENT, N_DP, N_HEAD, HEAD_COLS), LATENT ** -0.5, 0.25, ((1, 16), (2, 8)), jnp.float32),
        "moment_one": bell_draw(key_list[3], (LATENT, N_DP, N_HEAD, HEAD_COLS), 0.5, 4.0, ((1, 16), (2, 8)), jnp.float32),
        "moment_two": jnp.clip(jnp.exp(math.log(2.0) - 2.9957323 * jax.random.uniform(key_list[4], (LATENT, N_DP, N_HEAD, HEAD_COLS), jnp.float32) ** block_levels(key_list[4], (LATENT, N_DP, N_HEAD, HEAD_COLS), ((1, 16), (2, 8)), -0.2, 0.2)), 0.1, 2.0),
    }


def hadamard(length):
    row_index = jnp.arange(length, dtype=jnp.int32)[:, None]
    col_index = jnp.arange(length, dtype=jnp.int32)[None, :]
    common = jnp.bitwise_and(row_index, col_index)
    parity = jnp.zeros((length, length), jnp.int32)
    for position in range(length.bit_length()):
        parity = parity + jnp.bitwise_and(jnp.right_shift(common, position), 1)
    sign_table = 1.0 - 2.0 * jnp.bitwise_and(parity, 1).astype(jnp.float32)
    return sign_table / math.sqrt(length)

def reference(latent, out_grad, weight, moment_one, moment_two):
    rotation = hadamard(LATENT)
    weight_half = weight.astype(jnp.bfloat16).reshape(LATENT, -1)
    flat_grad = out_grad.reshape(TOKENS, -1)
    latent_grad = jnp.dot(flat_grad, weight_half.T, preferred_element_type=jnp.float32).astype(jnp.bfloat16)

    def shard_term(running, shard_index):
        shard_rows = lax.dynamic_slice_in_dim(latent, shard_index * TOK_DEV, TOK_DEV, 0)
        shard_grads = lax.dynamic_slice_in_dim(flat_grad, shard_index * TOK_DEV, TOK_DEV, 0)
        partial_value = jnp.dot(shard_rows.T, shard_grads, preferred_element_type=jnp.float32)
        rotated = jnp.dot(rotation, partial_value, precision=lax.Precision.HIGHEST)
        spread = jnp.sqrt(lax.optimization_barrier(jnp.mean(rotated * rotated, axis=0, keepdims=True)) + 1e-06)
        turned = jnp.clip(rotated, -2.0 * spread, 2.0 * spread).astype(jnp.bfloat16)
        turned = lax.optimization_barrier(turned)
        return (running + turned.astype(jnp.float32), None)
    start_sum = jnp.zeros((LATENT, N_DP * N_HEAD * HEAD_COLS), jnp.float32)
    summed, _ = lax.scan(shard_term, start_sum, jnp.arange(N_DP, dtype=jnp.int32))
    gradient = jnp.dot(rotation, summed, precision=lax.Precision.HIGHEST) * TOKENS ** (-0.5)
    gradient = gradient.reshape(weight.shape)
    new_moment_one = 0.9 * moment_one + 0.1 * gradient
    new_moment_two = 0.95 * moment_two + 0.05 * gradient * gradient
    update = new_moment_one / (1.0 - 0.9 ** 10) / (jnp.sqrt(new_moment_two / (1.0 - 0.95 ** 10)) + 1e-08)
    new_weight = weight - 0.001 * (update + 0.1 * weight)
    return (latent_grad, new_weight, new_moment_one, new_moment_two)
```

```python
import math

import jax
import jax.numpy as jnp
import numpy as np
from jax import lax
from jax.experimental import pallas as pl
from jax.experimental.pallas import tpu as pltpu
from jax.sharding import PartitionSpec as P


LATENT = 512
COLS = 256
NX, NZH, NC = 4, 2, 2
NZL, NY = 2, 4
TOK = 1024
TOKENS = 16384
BF = jnp.bfloat16
F32 = jnp.float32
VM = pl.BlockSpec(memory_space=pltpu.VMEM)
AXES = ("dp", "head")
EARLY = ((1, 1), (3, 1), (2, 1))
LATE = ((1, 0), (3, 0), (2, 0), (0, 1), (0, 0))
ORDER = ((0, 0), (1, 0), (3, 0), (2, 0), (0, 1), (1, 1), (3, 1), (2, 1))


def signs(length):
    i = np.arange(length)
    common = i[:, None] & i[None, :]
    parity = np.zeros_like(common)
    for position in range(length.bit_length()):
        parity += (common >> position) & 1
    return jnp.asarray(1 - 2 * (parity & 1), BF)


def shifted(value, dx=0, dz=0, dc=0, dl=0, dy=0):
    sizes = (NX, NZH, NC, NZL, NY)
    steps = (dx, dz, dc, dl, dy)
    pairs = []
    for source, place in enumerate(np.ndindex(*sizes)):
        target = [(p + d) % n for p, d, n in zip(place, steps, sizes)]
        pairs.append((source, int(np.ravel_multi_index(target, sizes))))
    return lax.ppermute(value, AXES, pairs)


def kernel(body, outs, count, grid=None, in_specs=None, limit=16, home=False):
    shape_of = jax.ShapeDtypeStruct if home else pltpu.VMEM
    return pl.pallas_call(
        body,
        grid=grid or (),
        in_specs=in_specs or [VM] * count,
        out_specs=[VM] * len(outs),
        out_shape=[shape_of(shape, dtype) for shape, dtype in outs],
        compiler_params=pltpu.CompilerParams(vmem_limit_bytes=limit << 20),
    )


def group_of(dx, dz, dc):
    me = lax.axis_index("dp")
    x, zh, c = me // (NZH * NC), lax.rem(me // NC, NZH), lax.rem(me, NC)
    return (lax.rem(x + dx, NX) * NZH + lax.rem(zh + dz, NZH)) * NC + lax.rem(c + dc, NC)


def halve_body(w_ref, o_ref):
    for half in range(2):
        rows = w_ref[pl.ds(half, LATENT, stride=2), :]
        o_ref[:, half * 128 : half * 128 + 128] = rows.astype(BF)


def swap_body(g_ref, o_ref):
    tile = g_ref.shape[0]
    at = pl.multiple_of(pl.program_id(0) * tile, tile)
    o_ref[:, pl.ds(at, tile), :] = jnp.swapaxes(g_ref[...], 0, 1)


def rotate_body(h_ref, l_ref, o_ref):
    rows = l_ref[...].reshape(TOK, LATENT)
    turned = lax.dot_general(h_ref[...], rows, (((1,), (1,)), ((), ())), preferred_element_type=F32)
    o_ref[...] = (turned * (1.0 / math.sqrt(LATENT))).astype(BF)


def turned_block(l_ref, g_ref, block):
    value = jnp.dot(l_ref[...], g_ref[block], preferred_element_type=F32)
    spread = 2.0 * jnp.sqrt(jnp.mean(value * value, axis=0, keepdims=True) + 1e-06)
    return jnp.clip(value, -spread, spread).astype(BF)


def give_body(places):
    def body(g_ref, l_ref, o_ref):
        for at, (dx, dz) in enumerate(places):
            o_ref[at] = turned_block(l_ref, g_ref, group_of(dx, dz, 1))

    return body


def keep_body(places):
    def body(g_ref, l_ref, r_ref, *o_refs):
        for at, ((dx, dz), o_ref) in enumerate(zip(places, o_refs)):
            mine = turned_block(l_ref, g_ref, group_of(dx, dz, 0)).astype(F32)
            o_ref[...] = (mine + r_ref[at].astype(F32)).astype(o_ref.dtype)

    return body


def latent_body(g_ref, *refs):
    w_refs, o_ref = refs[:16], refs[16]
    for part in range(2):
        total = None
        for at, (dx, dz) in enumerate(ORDER):
            for dc in range(2):
                term = lax.dot_general(
                    g_ref[group_of(dx, dz, dc), part * 512 : part * 512 + 512],
                    w_refs[2 * at + dc][...],
                    (((1,), (1,)), ((), ())),
                    preferred_element_type=F32,
                )
                total = term if total is None else total + term
        o_ref[part * 4 : part * 4 + 4] = total.astype(BF).reshape(4, 128, LATENT)


def update_body(h_ref, own, d_up, d_down, over, far, w_ref, a_ref, b_ref, nw_ref, na_ref, nb_ref):
    summed = own[...] + d_up[...].astype(F32) + d_down[...].astype(F32)
    summed = summed + over[...].astype(F32) + far[...].astype(F32)
    high = summed.astype(BF)
    low = (summed - high.astype(F32)).astype(BF)
    h = h_ref[...]
    grad = jnp.dot(h, high, preferred_element_type=F32) + jnp.dot(h, low, preferred_element_type=F32)
    grad = grad * (TOKENS ** (-0.5) / math.sqrt(LATENT))
    for half in range(2):
        rows = pl.ds(half, LATENT, stride=2)
        g = grad[:, half * 128 : half * 128 + 128]
        one = 0.9 * a_ref[rows, :] + 0.1 * g
        two = 0.95 * b_ref[rows, :] + 0.05 * g * g
        step = one / (1.0 - 0.9**10) / (jnp.sqrt(two / (1.0 - 0.95**10)) + 1e-08)
        w = w_ref[rows, :]
        na_ref[rows, :] = one
        nb_ref[rows, :] = two
        nw_ref[rows, :] = w - 0.001 * (step + 0.1 * w)


def join_body(*refs):
    total = refs[0][...].astype(F32)
    for r in refs[1:-1]:
        total = total + r[...].astype(F32)
    refs[-1][...] = total.astype(BF)


def run(body, outs, *operands, **more):
    return kernel(body, outs, len(operands), **more)(*operands)


def send(value, **steps):
    return shifted(value, **steps)


def step(latent, out_grad, weight, moment_one, moment_two):
    h = signs(LATENT)
    flat = (1024, 128)
    block = (LATENT, COLS)
    one = [(block, BF)]
    peers = NZL * NY

    rows = jnp.broadcast_to(latent[None], (peers, *latent.shape))
    rows = lax.all_to_all(rows, "head", 0, 0, tiled=True)

    (w0,) = run(halve_body, one, weight.reshape(flat))
    w = {(0, 0): w0}
    w[0, 1] = send(w0, dz=1)
    w[2, 0] = send(w0, dx=2)
    w[3, 0] = send(w0, dx=1)
    w[1, 0] = send(w0, dx=-1)
    w[3, 1] = send(w[0, 1], dx=1)
    w[1, 1] = send(w[0, 1], dx=-1)
    w[2, 1] = send(w[2, 0], dz=1)
    ws = []
    for place in ORDER:
        ws += [w[place], send(w[place], dc=1)]

    tile = 128
    (grads,) = run(
        swap_body,
        [((16, TOK, COLS), BF)],
        out_grad[:, :, 0, :],
        grid=(TOK // tile,),
        in_specs=[pl.BlockSpec((tile, 16, COLS), lambda i: (i, 0, 0))],
        limit=24,
    )

    (turn,) = run(rotate_body, [((LATENT, TOK), BF)], h, rows)
    (give,) = run(give_body(EARLY), [((3, *block), BF)], grads, turn)
    got_early = send(give, dc=1)
    (give,) = run(give_body(LATE), [((5, *block), BF)], grads, turn)
    got_late = send(give, dc=1)
    up, down, other = run(keep_body(EARLY), one * 3, grads, turn, got_early)
    up = send(up, dx=1)
    down = send(down, dx=-1)
    other = send(other, dz=1)
    d_up, d_down, far, over, own = run(
        keep_body(LATE), one * 2 + [(block, F32)] * 3, grads, turn, got_late
    )
    d_up = send(d_up, dx=1)
    d_down = send(d_down, dx=-1)
    (over,) = run(join_body, one, over, up, down)
    over = send(over, dz=1)
    (far,) = run(join_body, one, far, other)
    far = send(far, dx=2)

    (partial,) = run(latent_body, [((peers, 128, LATENT), BF)], grads, *ws)
    arrived = lax.all_to_all(partial, "head", 0, 0, tiled=True)
    latent_grad = arrived.astype(F32).sum(axis=0).astype(BF)

    states = [s.reshape(flat) for s in (weight, moment_one, moment_two)]
    new = run(
        update_body, [(flat, F32)] * 3, h, own, d_up, d_down, over, far, *states,
        limit=24, home=True,
    )
    new = [n.reshape(weight.shape) for n in new]
    return (latent_grad, *new)


def solution(mesh):
    state = P(None, "dp", "head", None)
    return jax.shard_map(
        step,
        mesh=mesh,
        in_specs=(P(("dp", "head"), None), P("dp", None, "head", None), state, state, state),
        out_specs=(P(("dp", "head"), None), state, state, state),
        check_vma=False,
    )
```

```python
import math

import jax
import jax.numpy as jnp
import numpy as np
from jax import lax
from jax.experimental import pallas as pl
from jax.experimental.pallas import tpu as pltpu
from jax.sharding import PartitionSpec as P


LATENT = 512
COLS = 256
NX, NZH, NC = 4, 2, 2
NZL, NY = 2, 4
TOK = 1024
TOKENS = 16384
BF = jnp.bfloat16
F32 = jnp.float32
VM = pl.BlockSpec(memory_space=pltpu.VMEM)
AXES = ("dp", "head")


def signs(length):
    i = np.arange(length)
    common = i[:, None] & i[None, :]
    parity = np.zeros_like(common)
    for position in range(length.bit_length()):
        parity += (common >> position) & 1
    return jnp.asarray(1 - 2 * (parity & 1), BF)


def shifted(value, dx=0, dz=0, dc=0, dl=0, dy=0, fan_x=0, fan_y=0):
    sizes = (NX, NZH, NC, NZL, NY)
    pairs = []
    for source, place in enumerate(np.ndindex(*sizes)):
        sign = 1 - 2 * place[2]
        steps = (dx + sign * fan_x, dz, dc, dl, dy + sign * fan_y)
        target = [(p + d) % n for p, d, n in zip(place, steps, sizes)]
        pairs.append((source, int(np.ravel_multi_index(target, sizes))))
    return lax.ppermute(value, AXES, pairs)


def kernel(body, outs, count, in_specs=None, scratch=(), limit=16, home=False):
    shape_of = jax.ShapeDtypeStruct if home else pltpu.VMEM
    return pl.pallas_call(
        body,
        in_specs=in_specs or [VM] * count,
        out_specs=[VM] * len(outs),
        out_shape=[shape_of(shape, dtype) for shape, dtype in outs],
        scratch_shapes=list(scratch),
        compiler_params=pltpu.CompilerParams(vmem_limit_bytes=limit << 20),
    )


def my_core():
    return lax.rem(lax.axis_index("dp"), NC)


def ahead(core):
    return 1 + 2 * core


def group_at(dx, dz, core):
    me = lax.axis_index("dp")
    x, zh = me // (NZH * NC), lax.rem(me // NC, NZH)
    return (lax.rem(x + dx, NX) * NZH + lax.rem(zh + dz, NZH)) * NC + core


def head_at(dl, dy):
    me = lax.axis_index("head")
    return lax.rem(me // NY + dl, NZL) * NY + lax.rem(me + dy, NY)


def front_body(h_hbm, l_hbm, w_hbm, o_ref, turn_ref, h_ref, l_ref, w_ref, sems):
    moves = zip((w_hbm, l_hbm, h_hbm), (w_ref, l_ref, h_ref))
    copies = [pltpu.make_async_copy(a, b, sems.at[i]) for i, (a, b) in enumerate(moves)]
    for copy in copies:
        copy.start()
    copies[0].wait()
    for half in range(2):
        rows = w_ref[pl.ds(half, LATENT, stride=2), :]
        o_ref[:, half * 128 : half * 128 + 128] = rows.astype(BF)
    copies[1].wait()
    copies[2].wait()
    turned = lax.dot_general(
        h_ref[...], l_ref[...], (((1,), (1,)), ((), ())), preferred_element_type=F32
    )
    turn_ref[...] = (turned * (1.0 / math.sqrt(LATENT))).astype(BF)


def swap_body(g_ref, o_ref, held, sems):
    parts = sems.shape[0]
    size = TOK // parts
    copies = [
        pltpu.make_async_copy(
            g_ref.at[pl.ds(part * size, size)], held.at[pl.ds(part * size, size)], sems.at[part]
        )
        for part in range(parts)
    ]
    for copy in copies:
        copy.start()
    for part, copy in enumerate(copies):
        copy.wait()
        rows = held[part * size : part * size + size]
        o_ref[:, part * size : part * size + size] = jnp.swapaxes(rows, 0, 1)


def pack_body(a_ref, b_ref, o_ref):
    o_ref[0] = a_ref[...]
    o_ref[1] = b_ref[...]


def cut_body(pair_ref, o_ref):
    o_ref[...] = pair_ref[0]


def place_body(own, pair, other, far, z_own, z_pair, z_other, z_far, o_ref):
    up, down = ahead(my_core()), ahead(1 - my_core())
    pieces = (
        (0, 0, own[...]), (0, down, pair[0]), (0, up, other[1]), (0, 2, far[...]),
        (1, 0, z_own[...]), (1, down, z_pair[0]), (1, up, z_other[1]), (1, 2, z_far[...]),
    )
    for dl, dy, turned in pieces:
        o_ref[:, pl.ds(pl.multiple_of(head_at(dl, dy) * 128, 128), 128)] = turned


def turned_block(l_ref, g_ref, block):
    value = jnp.dot(l_ref[...], g_ref[block], preferred_element_type=F32)
    spread = 2.0 * jnp.sqrt(jnp.mean(value * value, axis=0, keepdims=True) + 1e-06)
    return jnp.clip(value, -spread, spread).astype(BF)


def early(core):
    step = ahead(core)
    return [(step, 1, 0), (step, 1, 1), (2, 1, core)]


def late(core):
    step = ahead(core)
    return [(step, 0, 0), (step, 0, 1), (2, 0, core), (0, 1, core), (0, 0, core)]


def give_body(places):
    def body(g_ref, l_ref, o_ref):
        for at, place in enumerate(places(1 - my_core())):
            o_ref[at] = turned_block(l_ref, g_ref, group_at(*place))

    return body


def keep_body(places):
    def body(g_ref, l_ref, r_ref, pair, *single):
        for at, place in enumerate(places(my_core())):
            mine = turned_block(l_ref, g_ref, group_at(*place)).astype(F32) + r_ref[at].astype(F32)
            if at < 2:
                pair[at] = mine.astype(pair.dtype)
            else:
                single[at - 2][...] = mine.astype(single[at - 2].dtype)

    return body


def products(g_ref, terms, part):
    total = None
    for w, dx, dz, core in terms:
        rows = g_ref[group_at(dx, dz, core), part * 512 : part * 512 + 512]
        term = lax.dot_general(rows, w, (((1,), (1,)), ((), ())), preferred_element_type=F32)
        total = term if total is None else total + term
    return total


def latent_body(g_ref, p0, x, xs, f, fs, z, zs, zx, zxs, o_ref):
    core = my_core()
    rest = 1 - core
    up, down = ahead(core), ahead(rest)
    terms = [
        (p0[0], 0, 0, core), (p0[1], 0, 0, rest), (x[0], down, 0, core), (x[1], down, 0, rest),
        (xs[0], up, 0, rest), (xs[1], up, 0, core), (f[...], 2, 0, core), (fs[...], 2, 0, rest),
        (z[...], 0, 1, core), (zs[...], 0, 1, rest), (zx[0], down, 1, core), (zx[1], down, 1, rest),
        (zxs[0], up, 1, rest), (zxs[1], up, 1, core),
    ]
    for part in range(2):
        o_ref[part * 512 : part * 512 + 512] = products(g_ref, terms, part)


def finish_body(g_ref, zf, zfs, part_ref, o_ref):
    core = my_core()
    terms = [(zf[...], 2, 1, core), (zfs[...], 2, 1, 1 - core)]
    for part in range(2):
        total = part_ref[part * 512 : part * 512 + 512] + products(g_ref, terms, part)
        o_ref[part * 4 : part * 4 + 4] = total.astype(BF).reshape(4, 128, LATENT)


def total_body(r_ref, o_ref):
    total = r_ref[0].astype(F32)
    for peer in range(1, NZL * NY):
        total = total + r_ref[peer].astype(F32)
    o_ref[...] = total.astype(BF)


def join_pair_body(base, pair, other, o_ref):
    core = my_core()
    total = base[...] + pair[core].astype(F32) + other[core].astype(F32)
    o_ref[...] = total.astype(BF)


def update_body(h_ref, own, pair, other, over, far, w_ref, a_ref, b_ref, nw_ref, na_ref, nb_ref):
    core = my_core()
    summed = own[...] + pair[core].astype(F32) + other[core].astype(F32)
    summed = summed + over[...].astype(F32) + far[...].astype(F32)
    high = summed.astype(BF)
    low = (summed - high.astype(F32)).astype(BF)
    h = h_ref[...]
    grad = jnp.dot(h, high, preferred_element_type=F32) + jnp.dot(h, low, preferred_element_type=F32)
    grad = grad * (TOKENS ** (-0.5) / math.sqrt(LATENT))
    for half in range(2):
        rows = pl.ds(half, LATENT, stride=2)
        g = grad[:, half * 128 : half * 128 + 128]
        one = 0.9 * a_ref[rows, :] + 0.1 * g
        two = 0.95 * b_ref[rows, :] + 0.05 * g * g
        step = one / (1.0 - 0.9**10) / (jnp.sqrt(two / (1.0 - 0.95**10)) + 1e-08)
        w = w_ref[rows, :]
        na_ref[rows, :] = one
        nb_ref[rows, :] = two
        nw_ref[rows, :] = w - 0.001 * (step + 0.1 * w)


def join_body(*refs):
    total = refs[0][...].astype(F32)
    for r in refs[1:-1]:
        total = total + r[...].astype(F32)
    refs[-1][...] = total.astype(BF)


def run(body, outs, *operands, **more):
    return kernel(body, outs, len(operands), **more)(*operands)


def send(value, **steps):
    return shifted(value, **steps)


def step(latent, out_grad, weight, moment_one, moment_two):
    h = signs(LATENT)
    flat = (1024, 128)
    block = (LATENT, COLS)
    one = [(block, BF)]
    peers = NZL * NY

    far_off = [pltpu.with_memory_space_constraint(v, pltpu.HBM) for v in (h, latent, weight.reshape(flat))]
    w, turn = run(
        front_body,
        [(block, BF), ((LATENT, 128), BF)],
        *far_off,
        in_specs=[pl.BlockSpec(memory_space=pltpu.HBM)] * 3,
        scratch=[
            pltpu.VMEM((LATENT, LATENT), BF), pltpu.VMEM((128, LATENT), BF), pltpu.VMEM(flat, F32),
            pltpu.SemaphoreType.DMA((3,)),
        ],
    )
    rows_pair = [((2, LATENT, 128), BF)]
    (l_pair,) = run(pack_body, rows_pair, turn, send(turn, dc=1))
    l_z = send(turn, dl=1)
    l_y = send(l_pair, fan_y=1)
    l_ys = send(l_y, dc=1)
    (lz_pair,) = run(pack_body, rows_pair, l_z, send(l_z, dc=1))
    l_zy = send(lz_pair, fan_y=1)
    l_zys = send(l_zy, dc=1)
    l_2 = send(run(cut_body, [((LATENT, 128), BF)], l_y)[0], fan_y=1)
    l_2z = send(run(cut_body, [((LATENT, 128), BF)], l_zy)[0], fan_y=1)

    pair = [((2, *block), BF)]
    (w_pair,) = run(pack_body, pair, w, send(w, dc=1))
    w_z = send(w, dz=1)
    w_x = send(w_pair, fan_x=1)
    w_zs = send(w_z, dc=1)
    (wz_pair,) = run(pack_body, pair, w_z, w_zs)
    w_zx = send(wz_pair, fan_x=1)
    w_2 = send(run(cut_body, one, w_x)[0], fan_x=1)
    w_2z = send(run(cut_body, one, w_zx)[0], fan_x=1)
    ws = [
        w_pair, w_x, send(w_x, dc=1), w_2, send(w_2, dc=1), w_z, w_zs,
        w_zx, send(w_zx, dc=1),
    ]

    (grads,) = run(
        swap_body,
        [((16, TOK, COLS), BF)],
        pltpu.with_memory_space_constraint(out_grad[:, :, 0, :], pltpu.HBM),
        in_specs=[pl.BlockSpec(memory_space=pltpu.HBM)],
        scratch=[pltpu.VMEM((TOK, 16, COLS), BF), pltpu.SemaphoreType.DMA((8,))],
        limit=24,
    )

    (turn,) = run(place_body, [((LATENT, TOK), BF)], turn, l_y, l_ys, l_2, l_z, l_zy, l_zys, l_2z)
    (give,) = run(give_body(early), [((3, *block), BF)], grads, turn)
    got = send(give, dc=1)
    t_a, t_b = run(keep_body(early), pair + one, grads, turn, got)
    (give,) = run(give_body(late), [((5, *block), BF)], grads, turn)
    got = send(give, dc=1)
    t_d, far, over, own = run(keep_body(late), pair + [(block, F32)] * 3, grads, turn, got)
    t_a = send(t_a, fan_x=1)
    t_b = send(t_b, dz=1)
    t_d = send(t_d, fan_x=1)
    (over,) = run(join_pair_body, one, over, t_a, send(t_a, dc=1))
    over = send(over, dz=1)
    (far,) = run(join_body, one, far, t_b)
    far = send(far, dx=2)

    (partial,) = run(latent_body, [((TOK, LATENT), F32)], grads, *ws)
    (partial,) = run(
        finish_body, [((peers, 128, LATENT), BF)],
        grads, w_2z, send(w_2z, dc=1), partial,
    )
    arrived = lax.all_to_all(partial, "head", 0, 0, tiled=True)
    (latent_grad,) = run(total_body, [(latent.shape, BF)], arrived, home=True)

    states = [s.reshape(flat) for s in (weight, moment_one, moment_two)]
    new = run(
        update_body, [(flat, F32)] * 3, h, own, t_d, send(t_d, dc=1), over, far, *states,
        limit=24, home=True,
    )
    new = [n.reshape(weight.shape) for n in new]
    return (latent_grad, *new)


def solution(mesh):
    state = P(None, "dp", "head", None)
    return jax.shard_map(
        step,
        mesh=mesh,
        in_specs=(P(("dp", "head"), None), P("dp", None, "head", None), state, state, state),
        out_specs=(P(("dp", "head"), None), state, state, state),
        check_vma=False,
    )
```

```python
import math

import jax
import jax.numpy as jnp
import numpy as np
from jax import lax
from jax.experimental import pallas as pl
from jax.experimental.pallas import tpu as pltpu
from jax.sharding import PartitionSpec as P


LATENT = 512
COLS = 256
NX, NZH, NC = 4, 2, 2
NZL, NY = 2, 4
TOK = 1024
TOKENS = 16384
BF = jnp.bfloat16
F32 = jnp.float32
VM = pl.BlockSpec(memory_space=pltpu.VMEM)
AXES = ("dp", "head")


def signs(length):
    i = np.arange(length)
    common = i[:, None] & i[None, :]
    parity = np.zeros_like(common)
    for position in range(length.bit_length()):
        parity += (common >> position) & 1
    return jnp.asarray(1 - 2 * (parity & 1), BF)


def shifted(value, dx=0, dz=0, dc=0, dl=0, dy=0, fan_x=0, fan_y=0):
    sizes = (NX, NZH, NC, NZL, NY)
    pairs = []
    for source, place in enumerate(np.ndindex(*sizes)):
        sign = 1 - 2 * place[2]
        steps = (dx + sign * fan_x, dz, dc, dl, dy + sign * fan_y)
        target = [(p + d) % n for p, d, n in zip(place, steps, sizes)]
        pairs.append((source, int(np.ravel_multi_index(target, sizes))))
    return lax.ppermute(value, AXES, pairs)


def kernel(body, outs, count, in_specs=None, scratch=(), limit=16, home=False):
    shape_of = jax.ShapeDtypeStruct if home else pltpu.VMEM
    return pl.pallas_call(
        body,
        in_specs=in_specs or [VM] * count,
        out_specs=[VM] * len(outs),
        out_shape=[shape_of(shape, dtype) for shape, dtype in outs],
        scratch_shapes=list(scratch),
        compiler_params=pltpu.CompilerParams(vmem_limit_bytes=limit << 20),
    )


def my_core():
    return lax.rem(lax.axis_index("dp"), NC)


def ahead(core):
    return 1 + 2 * core


def group_at(dx, dz, core):
    me = lax.axis_index("dp")
    x, zh = me // (NZH * NC), lax.rem(me // NC, NZH)
    return (lax.rem(x + dx, NX) * NZH + lax.rem(zh + dz, NZH)) * NC + core


def head_at(dl, dy):
    me = lax.axis_index("head")
    return lax.rem(me // NY + dl, NZL) * NY + lax.rem(me + dy, NY)


def front_body(h_hbm, l_hbm, w_hbm, o_ref, turn_ref, h_ref, l_ref, w_ref, sems):
    moves = zip((w_hbm, l_hbm, h_hbm), (w_ref, l_ref, h_ref))
    copies = [pltpu.make_async_copy(a, b, sems.at[i]) for i, (a, b) in enumerate(moves)]
    for copy in copies:
        copy.start()
    copies[0].wait()
    for half in range(2):
        rows = w_ref[pl.ds(half, LATENT, stride=2), :]
        o_ref[:, half * 128 : half * 128 + 128] = rows.astype(BF)
    copies[1].wait()
    copies[2].wait()
    turned = lax.dot_general(
        h_ref[...], l_ref[...], (((1,), (1,)), ((), ())), preferred_element_type=F32
    )
    turn_ref[...] = (turned * (1.0 / math.sqrt(LATENT))).astype(BF)


def swap_body(g_ref, o_ref):
    size = 128
    for part in range(TOK // size):
        rows = g_ref[part * size : part * size + size]
        o_ref[:, part * size : part * size + size] = jnp.swapaxes(rows, 0, 1)


def pack_body(a_ref, b_ref, o_ref):
    o_ref[0] = a_ref[...]
    o_ref[1] = b_ref[...]


def pack_beside_body(g_hbm, a_ref, b_ref, o_ref):
    pack_body(a_ref, b_ref, o_ref)


def cut_body(pair_ref, o_ref):
    o_ref[...] = pair_ref[0]


def place_body(*refs):
    for place, ref in zip(((0, 0), (0, 3), (0, 1), (0, 2), (1, 0), (1, 3), (1, 1), (1, 2)), refs):
        at = pl.multiple_of(head_at(*place) * 128, 128)
        refs[-1][:, pl.ds(at, 128)] = ref[...]


def turned_block(l_ref, g_ref, block):
    value = jnp.dot(l_ref[...], g_ref[block], preferred_element_type=F32)
    spread = 2.0 * jnp.sqrt(jnp.mean(value * value, axis=0, keepdims=True) + 1e-06)
    return jnp.clip(value, -spread, spread).astype(BF)


def early(core):
    step = ahead(core)
    return [(step, 1, 0), (step, 1, 1), (2, 1, core)]


def late(core):
    step = ahead(core)
    return [(step, 0, 0), (step, 0, 1), (2, 0, core), (0, 1, core), (0, 0, core)]


def give_body(places):
    def body(g_ref, l_ref, o_ref):
        for at, place in enumerate(places(1 - my_core())):
            o_ref[at] = turned_block(l_ref, g_ref, group_at(*place))

    return body


def keep_body(places):
    def body(g_ref, l_ref, r_ref, pair, *single):
        for at, place in enumerate(places(my_core())):
            mine = turned_block(l_ref, g_ref, group_at(*place)).astype(F32) + r_ref[at].astype(F32)
            if at < 2:
                pair[at] = mine.astype(pair.dtype)
            else:
                single[at - 2][...] = mine.astype(single[at - 2].dtype)

    return body


def products(g_ref, terms, part):
    total = None
    for w, dx, dz, core in terms:
        rows = g_ref[group_at(dx, dz, core), part * 512 : part * 512 + 512]
        term = lax.dot_general(rows, w, (((1,), (1,)), ((), ())), preferred_element_type=F32)
        total = term if total is None else total + term
    return total


def latent_body(g_ref, p0, x, xs, f, fs, z, zs, zx, zxs, zf, zfs, *refs):
    core = my_core()
    rest = 1 - core
    up, down = ahead(core), ahead(rest)
    terms = [
        (p0[0], 0, 0, core), (p0[1], 0, 0, rest), (x[0], down, 0, core), (x[1], down, 0, rest),
        (xs[0], up, 0, rest), (xs[1], up, 0, core), (f[...], 2, 0, core), (fs[...], 2, 0, rest),
        (z[...], 0, 1, core), (zs[...], 0, 1, rest), (zx[0], down, 1, core), (zx[1], down, 1, rest),
        (zxs[0], up, 1, rest), (zxs[1], up, 1, core), (zf[...], 2, 1, core), (zfs[...], 2, 1, rest),
    ]
    for part in range(2):
        total = products(g_ref, terms, part)
        refs[-1][part * 4 : part * 4 + 4] = total.astype(BF).reshape(4, 128, LATENT)
    for dy, o_ref in zip((0, 1, 3, 2), refs):
        for dl in range(NZL):
            o_ref[dl] = refs[-1][head_at(dl, dy)]


def meet_body(own, up, down, far, near_ref, cross_ref):
    for dl, o_ref in enumerate((near_ref, cross_ref)):
        total = own[dl].astype(F32) + up[dl].astype(F32) + down[dl].astype(F32) + far[dl].astype(F32)
        o_ref[...] = total.astype(o_ref.dtype)


def total_body(near, cross, o_ref):
    o_ref[...] = (near[...] + cross[...].astype(F32)).astype(BF)


def join_pair_body(base, pair, other, o_ref):
    core = my_core()
    total = base[...].astype(F32) + pair[core].astype(F32) + other[core].astype(F32)
    o_ref[...] = total.astype(o_ref.dtype)


def update_body(h_ref, base, over, far, w_ref, a_ref, b_ref, nw_ref, na_ref, nb_ref):
    summed = base[...] + over[...].astype(F32) + far[...].astype(F32)
    high = summed.astype(BF)
    low = (summed - high.astype(F32)).astype(BF)
    h = h_ref[...]
    grad = jnp.dot(h, high, preferred_element_type=F32) + jnp.dot(h, low, preferred_element_type=F32)
    grad = grad * (TOKENS ** (-0.5) / math.sqrt(LATENT))
    for half in range(2):
        rows = pl.ds(half, LATENT, stride=2)
        g = grad[:, half * 128 : half * 128 + 128]
        one = 0.9 * a_ref[rows, :] + 0.1 * g
        two = 0.95 * b_ref[rows, :] + 0.05 * g * g
        step = one / (1.0 - 0.9**10) / (jnp.sqrt(two / (1.0 - 0.95**10)) + 1e-08)
        w = w_ref[rows, :]
        na_ref[rows, :] = one
        nb_ref[rows, :] = two
        nw_ref[rows, :] = w - 0.001 * (step + 0.1 * w)


def join_body(*refs):
    total = refs[0][...].astype(F32)
    for r in refs[1:-1]:
        total = total + r[...].astype(F32)
    refs[-1][...] = total.astype(BF)


def run(body, outs, *operands, **more):
    return kernel(body, outs, len(operands), **more)(*operands)


def send(value, **steps):
    return shifted(value, **steps)


def step(latent, out_grad, weight, moment_one, moment_two):
    h = signs(LATENT)
    flat = (1024, 128)
    block = (LATENT, COLS)
    one = [(block, BF)]

    far_off = [pltpu.with_memory_space_constraint(v, pltpu.HBM) for v in (h, latent, weight.reshape(flat))]
    w, turn = run(
        front_body,
        [(block, BF), ((LATENT, 128), BF)],
        *far_off,
        in_specs=[pl.BlockSpec(memory_space=pltpu.HBM)] * 3,
        scratch=[
            pltpu.VMEM((LATENT, LATENT), BF), pltpu.VMEM((128, LATENT), BF), pltpu.VMEM(flat, F32),
            pltpu.SemaphoreType.DMA((3,)),
        ],
    )
    l_z = send(turn, dl=1)
    l_up = send(turn, dy=1)
    l_dn = send(turn, dy=-1)
    l_2 = send(l_up, dy=1)
    lz_up = send(l_z, dy=1)
    lz_dn = send(l_z, dy=-1)
    lz_2 = send(lz_dn, dy=-1)
    rows = (turn, l_up, l_dn, l_2, l_z, lz_up, lz_dn, lz_2)

    pair = [((2, *block), BF)]
    (w_pair,) = run(
        pack_beside_body, pair,
        pltpu.with_memory_space_constraint(out_grad[:, :, 0, :], pltpu.HBM), w, send(w, dc=1),
        in_specs=[pl.BlockSpec(memory_space=pltpu.HBM), VM, VM],
    )
    w_z = send(w, dz=1)
    w_x = send(w_pair, fan_x=1)
    w_zs = send(w_z, dc=1)
    (wz_pair,) = run(pack_body, pair, w_z, w_zs)
    w_zx = send(wz_pair, fan_x=1)
    w_2 = send(run(cut_body, one, w_x)[0], fan_x=1)
    w_2z = send(w_2, dz=1)
    ws = [
        w_pair, w_x, send(w_x, dc=1), w_2, send(w_2, dc=1), w_z, w_zs,
        w_zx, send(w_zx, dc=1),
    ]

    (grads,) = run(swap_body, [((16, TOK, COLS), BF)], out_grad[:, :, 0, :])

    (turn,) = run(place_body, [((LATENT, TOK), BF)], *rows)
    (give,) = run(give_body(early), [((3, *block), BF)], grads, turn)
    got = send(give, dc=1)
    t_a, t_b = run(keep_body(early), pair + one, grads, turn, got)
    (give,) = run(give_body(late), [((5, *block), BF)], grads, turn)
    got = send(give, dc=1)
    t_d, far, over, own = run(keep_body(late), pair + one * 3, grads, turn, got)
    t_a = send(t_a, fan_x=1)
    t_b = send(t_b, dz=1)
    t_d = send(t_d, fan_x=1)
    (over,) = run(join_pair_body, one, over, t_a, send(t_a, dc=1))
    over = send(over, dz=1)
    (far,) = run(join_body, one, far, t_b)
    far = send(far, dx=2)

    piece = (128, LATENT)
    s_own, s_up, s_dn, s_2 = run(
        latent_body, [((NZL, *piece), BF)] * 4,
        grads, *ws, w_2z, send(w_2z, dc=1),
        scratch=[pltpu.VMEM((NZL * NY, *piece), BF)],
    )
    s_2 = send(s_2, dy=2)
    s_up = send(s_up, dy=1)
    s_dn = send(s_dn, dy=-1)
    near, cross = run(meet_body, [(piece, F32), (piece, BF)], s_own, s_up, s_dn, s_2)
    cross = send(cross, dl=1)
    (latent_grad,) = run(total_body, [(piece, BF)], near, cross, home=True)

    (own,) = run(join_pair_body, [(block, F32)], own, t_d, send(t_d, dc=1))
    states = [s.reshape(flat) for s in (weight, moment_one, moment_two)]
    new = run(
        update_body, [(flat, F32)] * 3, h, own, over, far, *states,
        limit=24, home=True,
    )
    new = [n.reshape(weight.shape) for n in new]
    return (latent_grad, *new)


def solution(mesh):
    state = P(None, "dp", "head", None)
    return jax.shard_map(
        step,
        mesh=mesh,
        in_specs=(P(("dp", "head"), None), P("dp", None, "head", None), state, state, state),
        out_specs=(P(("dp", "head"), None), state, state, state),
        check_vma=False,
    )
```

```python
import math

import jax
import jax.numpy as jnp
import numpy as np
from jax import lax
from jax.experimental import pallas as pl
from jax.experimental.pallas import tpu as pltpu
from jax.sharding import PartitionSpec as P


LATENT = 512
COLS = 256
NX, NZH, NC = 4, 2, 2
NZL, NY = 2, 4
TOK = 1024
TOKENS = 16384
BF = jnp.bfloat16
F32 = jnp.float32
VM = pl.BlockSpec(memory_space=pltpu.VMEM)
AXES = ("dp", "head")


def signs(length):
    i = np.arange(length)
    common = i[:, None] & i[None, :]
    parity = np.zeros_like(common)
    for position in range(length.bit_length()):
        parity += (common >> position) & 1
    return jnp.asarray(1 - 2 * (parity & 1), BF)


def shifted(value, dx=0, dz=0, dc=0, dl=0, dy=0, fan_x=0, fan_y=0):
    sizes = (NX, NZH, NC, NZL, NY)
    pairs = []
    for source, place in enumerate(np.ndindex(*sizes)):
        sign = 1 - 2 * place[2]
        steps = (dx + sign * fan_x, dz, dc, dl, dy + sign * fan_y)
        target = [(p + d) % n for p, d, n in zip(place, steps, sizes)]
        pairs.append((source, int(np.ravel_multi_index(target, sizes))))
    return lax.ppermute(value, AXES, pairs)


def kernel(body, outs, count, in_specs=None, scratch=(), limit=16, home=False):
    shape_of = jax.ShapeDtypeStruct if home else pltpu.VMEM
    return pl.pallas_call(
        body,
        in_specs=in_specs or [VM] * count,
        out_specs=[VM] * len(outs),
        out_shape=[shape_of(shape, dtype) for shape, dtype in outs],
        scratch_shapes=list(scratch),
        compiler_params=pltpu.CompilerParams(vmem_limit_bytes=limit << 20),
    )


def my_core():
    return lax.rem(lax.axis_index("dp"), NC)


def ahead(core):
    return 1 + 2 * core


def group_at(dx, dz, core):
    me = lax.axis_index("dp")
    x, zh = me // (NZH * NC), lax.rem(me // NC, NZH)
    return (lax.rem(x + dx, NX) * NZH + lax.rem(zh + dz, NZH)) * NC + core


def head_at(dl, dy):
    me = lax.axis_index("head")
    return lax.rem(me // NY + dl, NZL) * NY + lax.rem(me + dy, NY)


def front_body(h_hbm, l_hbm, w_hbm, o_ref, turn_ref, h_ref, l_ref, w_ref, sems):
    moves = zip((w_hbm, l_hbm, h_hbm), (w_ref, l_ref, h_ref))
    copies = [pltpu.make_async_copy(a, b, sems.at[i]) for i, (a, b) in enumerate(moves)]
    for copy in copies:
        copy.start()
    copies[0].wait()
    for half in range(2):
        rows = w_ref[pl.ds(half, LATENT, stride=2), :]
        o_ref[:, half * 128 : half * 128 + 128] = rows.astype(BF)
    copies[1].wait()
    copies[2].wait()
    turned = lax.dot_general(
        h_ref[...], l_ref[...], (((1,), (1,)), ((), ())), preferred_element_type=F32
    )
    turn_ref[...] = (turned * (1.0 / math.sqrt(LATENT))).astype(BF)


def swap_body(g_ref, o_ref):
    size = 128
    for part in range(TOK // size):
        rows = g_ref[part * size : part * size + size]
        o_ref[:, part * size : part * size + size] = jnp.swapaxes(rows, 0, 1)


def pack_body(a_ref, b_ref, o_ref):
    o_ref[0] = a_ref[...]
    o_ref[1] = b_ref[...]


def pack_beside_body(g_hbm, a_ref, b_ref, o_ref):
    pack_body(a_ref, b_ref, o_ref)


def pack_more_body(pair_ref, b_ref, o_ref):
    o_ref[:2] = pair_ref[...]
    o_ref[2] = b_ref[...]


def cut_body(pair_ref, o_ref):
    o_ref[...] = pair_ref[0]


def place_body(*refs):
    for dy, ref in zip((0, 3, 2, 1), refs):
        for dl in range(NZL):
            at = pl.multiple_of(head_at(dl, dy) * 128, 128)
            refs[-1][:, pl.ds(at, 128)] = ref[dl]


def turned_block(l_ref, g_ref, block):
    value = jnp.dot(l_ref[...], g_ref[block], preferred_element_type=F32)
    spread = 2.0 * jnp.sqrt(jnp.mean(value * value, axis=0, keepdims=True) + 1e-06)
    return jnp.clip(value, -spread, spread).astype(BF)


def early(core):
    step = ahead(core)
    return [(step, 1, 0), (step, 1, 1), (2, 1, core)]


def late(core):
    step = ahead(core)
    return [(step, 0, 0), (step, 0, 1), (2, 0, core), (0, 1, core), (0, 0, core)]


def give_body(places):
    def body(g_ref, l_ref, o_ref):
        for at, place in enumerate(places(1 - my_core())):
            o_ref[at] = turned_block(l_ref, g_ref, group_at(*place))

    return body


def keep_body(places):
    def body(g_ref, l_ref, r_ref, pair, *single):
        for at, place in enumerate(places(my_core())):
            mine = turned_block(l_ref, g_ref, group_at(*place)).astype(F32) + r_ref[at].astype(F32)
            if at < 2:
                pair[at] = mine.astype(pair.dtype)
            else:
                single[at - 2][...] = mine.astype(single[at - 2].dtype)

    return body


def products(g_ref, terms, part):
    total = None
    for w, dx, dz, core in terms:
        rows = g_ref[group_at(dx, dz, core), part * 512 : part * 512 + 512]
        term = lax.dot_general(rows, w, (((1,), (1,)), ((), ())), preferred_element_type=F32)
        total = term if total is None else total + term
    return total


def latent_body(g_ref, p0, x, xs, z, zs, zx, zxs, zf, zfs, *refs):
    core = my_core()
    rest = 1 - core
    up, down = ahead(core), ahead(rest)
    terms = [
        (p0[0], 0, 0, core), (p0[1], 0, 0, rest), (x[0], down, 0, core), (x[1], down, 0, rest),
        (xs[0], up, 0, rest), (xs[1], up, 0, core), (x[2], 2, 0, core), (xs[2], 2, 0, rest),
        (z[...], 0, 1, core), (zs[...], 0, 1, rest), (zx[0], down, 1, core), (zx[1], down, 1, rest),
        (zxs[0], up, 1, rest), (zxs[1], up, 1, core), (zf[...], 2, 1, core), (zfs[...], 2, 1, rest),
    ]
    for part in range(2):
        total = products(g_ref, terms, part)
        refs[-1][part * 4 : part * 4 + 4] = total.astype(BF).reshape(4, 128, LATENT)
    for dy, o_ref in zip((0, 1, 3, 2), refs):
        for dl in range(NZL):
            o_ref[dl] = refs[-1][head_at(dl, dy)]


def meet_body(own, up, down, far, near_ref, cross_ref):
    for dl, o_ref in enumerate((near_ref, cross_ref)):
        total = own[dl].astype(F32) + up[dl].astype(F32) + down[dl].astype(F32) + far[dl].astype(F32)
        o_ref[...] = total.astype(o_ref.dtype)


def total_body(near, cross, o_ref):
    o_ref[...] = (near[...] + cross[...].astype(F32)).astype(BF)


def join_pair_body(base, pair, other, o_ref):
    core = my_core()
    total = base[...].astype(F32) + pair[core].astype(F32) + other[core].astype(F32)
    o_ref[...] = total.astype(o_ref.dtype)


def update_body(h_ref, base, over, far, w_ref, a_ref, b_ref, nw_ref, na_ref, nb_ref):
    summed = base[...] + over[...].astype(F32) + far[...].astype(F32)
    high = summed.astype(BF)
    low = (summed - high.astype(F32)).astype(BF)
    h = h_ref[...]
    grad = jnp.dot(h, high, preferred_element_type=F32) + jnp.dot(h, low, preferred_element_type=F32)
    grad = grad * (TOKENS ** (-0.5) / math.sqrt(LATENT))
    for half in range(2):
        rows = pl.ds(half, LATENT, stride=2)
        g = grad[:, half * 128 : half * 128 + 128]
        one = 0.9 * a_ref[rows, :] + 0.1 * g
        two = 0.95 * b_ref[rows, :] + 0.05 * g * g
        step = one / (1.0 - 0.9**10) / (jnp.sqrt(two / (1.0 - 0.95**10)) + 1e-08)
        w = w_ref[rows, :]
        na_ref[rows, :] = one
        nb_ref[rows, :] = two
        nw_ref[rows, :] = w - 0.001 * (step + 0.1 * w)


def join_body(*refs):
    total = refs[0][...].astype(F32)
    for r in refs[1:-1]:
        total = total + r[...].astype(F32)
    refs[-1][...] = total.astype(BF)


def run(body, outs, *operands, **more):
    return kernel(body, outs, len(operands), **more)(*operands)


def send(value, **steps):
    return shifted(value, **steps)


def step(latent, out_grad, weight, moment_one, moment_two):
    h = signs(LATENT)
    flat = (1024, 128)
    block = (LATENT, COLS)
    one = [(block, BF)]

    far_off = [pltpu.with_memory_space_constraint(v, pltpu.HBM) for v in (h, latent, weight.reshape(flat))]
    w, turn = run(
        front_body,
        [(block, BF), ((LATENT, 128), BF)],
        *far_off,
        in_specs=[pl.BlockSpec(memory_space=pltpu.HBM)] * 3,
        scratch=[
            pltpu.VMEM((LATENT, LATENT), BF), pltpu.VMEM((128, LATENT), BF), pltpu.VMEM(flat, F32),
            pltpu.SemaphoreType.DMA((3,)),
        ],
    )
    l_z = send(turn, dl=1)
    (both,) = run(pack_body, [((2, LATENT, 128), BF)], turn, l_z)
    l_up = send(both, dy=1)
    l_dn = send(both, dy=-1)
    l_2 = send(both, dy=2)

    pair = [((2, *block), BF)]
    (w_pair,) = run(
        pack_beside_body, pair,
        pltpu.with_memory_space_constraint(out_grad[:, :, 0, :], pltpu.HBM), w, send(w, dc=1),
        in_specs=[pl.BlockSpec(memory_space=pltpu.HBM), VM, VM],
    )
    w_z = send(w, dz=1)
    w_x = send(w_pair, fan_x=1)
    w_zs = send(w_z, dc=1)
    (wz_pair,) = run(pack_body, pair, w_z, w_zs)
    w_zx = send(wz_pair, fan_x=1)
    w_2 = send(run(cut_body, one, w_x)[0], fan_x=1)
    w_2z = send(w_2, dz=1)
    (w_row,) = run(pack_more_body, [((3, *block), BF)], w_x, w_2)
    ws = [w_pair, w_row, send(w_row, dc=1), w_z, w_zs, w_zx, send(w_zx, dc=1)]

    (grads,) = run(swap_body, [((16, TOK, COLS), BF)], out_grad[:, :, 0, :])

    (turn,) = run(place_body, [((LATENT, TOK), BF)], both, l_up, l_2, l_dn)
    (give,) = run(give_body(early), [((3, *block), BF)], grads, turn)
    got = send(give, dc=1)
    t_a, t_b = run(keep_body(early), pair + one, grads, turn, got)
    (give,) = run(give_body(late), [((5, *block), BF)], grads, turn)
    got = send(give, dc=1)
    t_d, far, over, own = run(keep_body(late), pair + one * 3, grads, turn, got)
    t_a = send(t_a, fan_x=1)
    t_b = send(t_b, dz=1)
    t_d = send(t_d, fan_x=1)
    (over,) = run(join_pair_body, one, over, t_a, send(t_a, dc=1))
    over = send(over, dz=1)
    (far,) = run(join_body, one, far, t_b)
    far = send(far, dx=2)

    piece = (128, LATENT)
    s_own, s_up, s_dn, s_2 = run(
        latent_body, [((NZL, *piece), BF)] * 4,
        grads, *ws, w_2z, send(w_2z, dc=1),
        scratch=[pltpu.VMEM((NZL * NY, *piece), BF)],
    )
    s_2 = send(s_2, dy=2)
    s_up = send(s_up, dy=1)
    s_dn = send(s_dn, dy=-1)
    near, cross = run(meet_body, [(piece, F32), (piece, BF)], s_own, s_up, s_dn, s_2)
    cross = send(cross, dl=1)
    (latent_grad,) = run(total_body, [(piece, BF)], near, cross, home=True)

    (own,) = run(join_pair_body, [(block, F32)], own, t_d, send(t_d, dc=1))
    states = [s.reshape(flat) for s in (weight, moment_one, moment_two)]
    new = run(
        update_body, [(flat, F32)] * 3, h, own, over, far, *states,
        limit=24, home=True,
    )
    new = [n.reshape(weight.shape) for n in new]
    return (latent_grad, *new)


def solution(mesh):
    state = P(None, "dp", "head", None)
    return jax.shard_map(
        step,
        mesh=mesh,
        in_specs=(P(("dp", "head"), None), P("dp", None, "head", None), state, state, state),
        out_specs=(P(("dp", "head"), None), state, state, state),
        check_vma=False,
    )
```
